512 devices in a mesh: pb: 16 (over y, core), ka: 32 (over x, z).
Axes of the slice: x: 4, y: 8, z: 8, core: 2. Of those that a mesh axis runs over, the one named last changes fastest.
Arguments:
- coupling: bfloat16 [16, 1728, 2, 1600], P('pb', 'ka'), may hold values from -6 to 6
- rot_k: bfloat16 [1728, 2, 1600], P('ka'), may hold values from -0.625 to 0.625
- rot_kq: bfloat16 [16, 1728, 2, 1600], P('pb', 'ka'), may hold values from -0.625 to 0.625
- r_elec: int32 [2048, 3], replicated, may hold values from -6 to 6
- degen: int32 [2048], replicated, may hold values from 1 to 8
- reader: int32 [2048, 1], replicated, may hold values from 0 to 31; in each aligned block of 2048 rows (0 to 2047, 2048 to 4095, ...) at most 128 rows name the same one
- r_phon: int32 [32, 3], replicated, may hold values from -3 to 3
Outputs:
- wannier: float32 [32, 2, 1600, 4096], P(None, None, 'pb', 'ka')
The draws below stay inside these ranges and needn't reach their ends.
Inputs may be any that keep to these rules, and one draw needn't show every extreme that they name: Each reader is named by at most 128 lattice vectors, and one reader by exactly 128.
All inputs are finite; a program needn't handle non-finite values.
Results may differ from the reference program's by a relative error of at most 0.0056.
Values may be sent and summed in bfloat16 or wider, within the bound.
A program may use at most 128 MiB of HBM per device.

```python
import math
import jax
import jax.numpy as jnp
import numpy as np
from jax import lax

W = 40
WW = 1600
KGRID = 12
NK = 1728
QGRID = 6
NQ = 16
NRE = 2048
NRP = 32
READERS = 32
MOST = 128
N_KA = 32


def with_ends(entries, stream_key, smallest, top_value):
    index_at = [jax.random.randint(jax.random.fold_in(stream_key, axis), (), 0, length) for axis, length in enumerate(entries.shape)]
    main_axis = entries.shape.index(max(entries.shape))
    neighbour = index_at[:main_axis] + [(index_at[main_axis] + 1) % entries.shape[main_axis]] + index_at[main_axis + 1:]
    return entries.at[tuple(index_at)].set(smallest).at[tuple(neighbour)].set(top_value)


def level_of(own_key, dims, split, low, high):
    gain = 1.0
    for dim, shards_of in split:
        heights = jax.random.uniform(jax.random.fold_in(jax.random.fold_in(own_key, 6), dim), (shards_of,), jnp.float32, low / len(split), high / len(split))
        gain = gain * jnp.repeat(jnp.exp(heights), dims[dim] // shards_of).reshape((-1,) + (1,) * (len(dims) - 1 - dim))
    return gain


def shared_out(key, own, number, rows, amount, top, bound, skew):
    sequence = jax.random.permutation(key, amount)
    heavy_load, ordinary = portions_of(amount, rows * top, bound, skew, True), portions_of(amount, rows * top, bound, skew, False)
    places = jnp.arange(amount)

    def named(lengths, rotation):
        used = int((lengths > 0).sum())
        fixed = max(1, used // 4)
        moved = fixed + (places - fixed + rotation * (used - fixed)) % max(1, amount - fixed)
        return jnp.zeros((amount,), jnp.int32).at[sequence[jnp.where(places < fixed, places, moved)]].set(jnp.asarray(lengths, jnp.int32))

    lengths = jnp.where(number % 4 == 0, named(heavy_load, number // 4), named(ordinary, number - number // 4 - 1))
    mixed = jax.random.permutation(jax.random.fold_in(own, 3), amount)
    source_of, taker = mixed[0:amount // 2 * 2:2], mixed[1:amount // 2 * 2:2]
    margin = jnp.minimum(lengths[source_of] - 1, bound - lengths[taker]) // 2
    margin = jnp.where((source_of == sequence[0]) | (taker == sequence[0]) | (lengths[taker] == 0), 0, jnp.maximum(margin, 0))
    moved = jax.random.randint(jax.random.fold_in(own, 4), (amount // 2,), 0, 1 << 20) % (margin + 1)
    lengths = lengths.at[source_of].add(-moved).at[taker].add(moved)
    members = jnp.searchsorted(jnp.cumsum(lengths), jnp.arange(rows * top), side="right").astype(jnp.int32)
    listing = members.reshape(top, rows).T
    listing = listing[jax.random.permutation(jax.random.fold_in(own, 1), rows)]
    rotation = jax.random.randint(jax.random.fold_in(own, 2), (rows, 1), 0, top)
    return jnp.take_along_axis(listing, (jnp.arange(top)[None, :] + rotation) % top, axis=1)


def portions_of(amount, total, bound, lean, full):
    loads = [(1 << 20) // math.isqrt(standing ** lean) + 1 for standing in range(1, amount + 1)]
    largest = bound if full else min(bound, max(-(-total // amount), total * loads[0] // sum(loads)))
    least = 1 if total - largest >= amount - 1 else 0
    given, rest = [largest] + [least] * (amount - 1), total - largest - least * (amount - 1)
    while rest > 0:
        movable = [i for i in range(1, amount) if given[i] < largest] or [i for i in range(1, amount) if given[i] < bound]
        mass, left = sum([loads[i] for i in movable]), rest
        for i in movable:
            extra = min(bound - given[i], max(1, left * loads[i] // mass), rest)
            given[i] = given[i] + extra
            rest = rest - extra
    return np.array(given)


def centred(own_key, extent, scale, reach, cuts=(), kind=jnp.bfloat16):
    level = level_of(own_key, extent, cuts, -0.22, 0.18) if cuts else 1.0
    values = jax.random.normal(own_key, extent, jnp.float32) * scale * level
    return jnp.minimum(jnp.maximum(values, -reach), reach).astype(kind)


def setup_inputs(seed: int = 0) -> dict:
    seeds = jax.random.split(jax.random.key(seed), 8)
    coupling = centred(seeds[0], (NQ, NK, 2, WW), 1.0, 6.0, ((0, 16), (1, 32)))
    rot_k = centred(seeds[1], (NK, 2, WW), (2 * W) ** -0.5, 0.625, ((0, 32),))
    rot_kq = centred(seeds[2], (NQ, NK, 2, WW), (2 * W) ** -0.5, 0.625, ((0, 16), (1, 32)))
    r_elec = with_ends(jax.random.randint(seeds[3], (NRE, 3), -6, 7), jax.random.fold_in(seeds[3], 1), -6, 6).astype(jnp.int32)
    degen = with_ends(jax.random.randint(seeds[4], (NRE,), 1, 9), jax.random.fold_in(seeds[4], 1), 1, 8).astype(jnp.int32)
    reader_keys = jax.random.split(jax.random.fold_in(seeds[5], 1), NRE // NRE)
    reader_turns = jax.random.permutation(jax.random.fold_in(seeds[5], 3), NRE // NRE)
    reader = jax.vmap(lambda own, number: shared_out(jax.random.fold_in(seeds[5], 2), own, number, NRE, READERS, 1, MOST, 1))(reader_keys, reader_turns).reshape((NRE, 1))
    r_phon = with_ends(jax.random.randint(seeds[6], (NRP, 3), -3, 4), jax.random.fold_in(seeds[6], 1), -3, 3).astype(jnp.int32)
    return dict(coupling=coupling, rot_k=rot_k, rot_kq=rot_kq, r_elec=r_elec, degen=degen, reader=reader, r_phon=r_phon)


def angle_tables(vectors, start, count, grid):
    index = start + jnp.arange(count, dtype=jnp.int32)
    first = index // (grid * grid)
    second = (index // grid) % grid
    third = index % grid
    inner = vectors[:, 0:1] * first[None, :] + vectors[:, 1:2] * second[None, :] + vectors[:, 2:3] * third[None, :]
    angle = jnp.mod(inner, grid).astype(jnp.float32) * (2.0 * math.pi / grid)
    return jnp.cos(angle).astype(jnp.bfloat16), jnp.sin(angle).astype(jnp.bfloat16)


def combine_parts(cosine, sine, z_real, z_imag):
    joined = jnp.concatenate([z_real, z_imag], axis=1)
    first = jnp.dot(cosine, joined, preferred_element_type=jnp.float32)
    second = jnp.dot(sine, joined, preferred_element_type=jnp.float32)
    width = z_real.shape[1]
    return first[:, :width] + second[:, width:], first[:, width:] - second[:, :width]


def slot_tables(reader, degen, readers, most):
    reader_row = reader[:, 0]
    member = (reader_row[:, None] == jnp.arange(readers, dtype=jnp.int32)[None, :]).astype(jnp.int32)
    ranking = jnp.sum((jnp.cumsum(member, axis=0) - 1) * member, axis=1)
    position = reader_row * most + ranking
    source_row = jnp.full((readers * most,), -1, jnp.int32).at[position].set(jnp.arange(reader_row.shape[0], dtype=jnp.int32))
    usable = source_row >= 0
    source_row = jnp.maximum(source_row, 0)
    inverse_deg = jnp.where(usable, 1.0 / degen[source_row].astype(jnp.float32), jnp.float32(0.0)).astype(jnp.float32)
    return position, source_row, usable, inverse_deg


def rotate_one(pair, rot_k):
    coupling_q, rot_q = pair
    g_mat = coupling_q.astype(jnp.float32).reshape(NK, 2, W, W)
    u_mat = rot_k.astype(jnp.float32).reshape(NK, 2, W, W)
    v_mat = rot_q.astype(jnp.float32).reshape(NK, 2, W, W)
    spec = 'kab,kbn->kan'
    x_real = jnp.einsum(spec, g_mat[:, 0], u_mat[:, 0]) - jnp.einsum(spec, g_mat[:, 1], u_mat[:, 1])
    x_imag = jnp.einsum(spec, g_mat[:, 0], u_mat[:, 1]) + jnp.einsum(spec, g_mat[:, 1], u_mat[:, 0])
    x_real = lax.optimization_barrier(x_real.astype(jnp.bfloat16)).astype(jnp.float32)
    x_imag = lax.optimization_barrier(x_imag.astype(jnp.bfloat16)).astype(jnp.float32)
    spec_two = 'kam,kan->kmn'
    y_real = jnp.einsum(spec_two, v_mat[:, 0], x_real) + jnp.einsum(spec_two, v_mat[:, 1], x_imag)
    y_imag = jnp.einsum(spec_two, v_mat[:, 0], x_imag) - jnp.einsum(spec_two, v_mat[:, 1], x_real)
    return jnp.stack([y_real, y_imag], 1).reshape(NK, 2, WW).astype(jnp.bfloat16)


def reference(coupling, rot_k, rot_kq, r_elec, degen, reader, r_phon):
    rotated = lax.map(lambda pair: rotate_one(pair, rot_k), (coupling, rot_kq))
    z_real = rotated[:, :, 0].transpose(1, 0, 2).reshape(NK, NQ * WW)
    z_imag = rotated[:, :, 1].transpose(1, 0, 2).reshape(NK, NQ * WW)
    block = math.gcd(NRE, 512)
    scale = NK ** -0.5

    def transform(vectors):
        cosine, sine = angle_tables(vectors, 0, NK, KGRID)
        real_part, imag_part = combine_parts(cosine, sine, z_real, z_imag)
        stacked = jnp.stack([real_part.reshape(block, NQ, WW), imag_part.reshape(block, NQ, WW)], 2)
        return (stacked * scale).astype(jnp.bfloat16)

    wigner = lax.map(transform, r_elec.reshape(NRE // block, block, 3)).reshape(NRE, NQ, 2, WW)
    position, source_row, usable, inverse_deg = slot_tables(reader, degen, N_KA, MOST)
    q_cos, q_sin = angle_tables(r_phon, 0, NQ, QGRID)

    def reader_block(args):
        rows, keep, inverse = args
        picked = jnp.where(keep[:, None, None, None], wigner[rows], jnp.bfloat16(0.0))
        flat = picked.transpose(1, 0, 2, 3).reshape(NQ, MOST * 2 * WW)
        c_part = jnp.dot(q_cos, flat, preferred_element_type=jnp.float32).reshape(NRP, MOST, 2, WW)
        s_part = jnp.dot(q_sin, flat, preferred_element_type=jnp.float32).reshape(NRP, MOST, 2, WW)
        real_out = c_part[:, :, 0] + s_part[:, :, 1]
        imag_out = c_part[:, :, 1] - s_part[:, :, 0]
        result = jnp.stack([real_out, imag_out], 1).transpose(0, 1, 3, 2)
        return result * (inverse * NQ ** -0.5)[None, None, None, :]

    blocks = lax.map(reader_block, (source_row.reshape(N_KA, MOST), usable.reshape(N_KA, MOST), inverse_deg.reshape(N_KA, MOST)))
    return blocks.transpose(1, 2, 3, 0, 4).reshape(NRP, 2, WW, N_KA * MOST)
```

```python
import math

import jax
import jax.numpy as jnp
import numpy as np
from jax import lax
from jax.experimental import pallas as pl
from jax.experimental.pallas import tpu as pltpu
from jax.sharding import PartitionSpec as P

W = 40
KGRID = 12
QGRID = 6
READERS = 32
MOST = 128
PLANE = KGRID * KGRID
ROWS = 1792
VMEM = pl.BlockSpec(memory_space=pltpu.VMEM)


def plane_table():
    index = np.arange(PLANE)
    inner = np.outer(index // KGRID, index // KGRID) + np.outer(index % KGRID, index % KGRID)
    angle = (inner % KGRID) * (2.0 * math.pi / KGRID)
    cosine, sine = np.cos(angle), np.sin(angle)
    return np.block([[cosine, sine], [-sine, cosine]]).astype(np.float32).astype(jnp.bfloat16)


def product(spec, left, right):
    return jnp.einsum(spec, left, right, preferred_element_type=jnp.float32)


def rotate(coupling, rot_k, rot_kq):
    k_local = coupling.shape[1]
    g_mat = coupling.reshape(k_local, 2, W, W)
    u_mat = rot_k.reshape(k_local, 2, W, W)
    v_mat = rot_kq.reshape(k_local, 2, W, W)
    spec = "kab,kbn->kan"
    x_real = product(spec, g_mat[:, 0], u_mat[:, 0]) - product(spec, g_mat[:, 1], u_mat[:, 1])
    x_imag = product(spec, g_mat[:, 0], u_mat[:, 1]) + product(spec, g_mat[:, 1], u_mat[:, 0])
    x_real = x_real.astype(jnp.bfloat16)
    x_imag = x_imag.astype(jnp.bfloat16)
    spec_two = "kam,kan->kmn"
    y_real = product(spec_two, v_mat[:, 0], x_real) + product(spec_two, v_mat[:, 1], x_imag)
    y_imag = product(spec_two, v_mat[:, 0], x_imag) - product(spec_two, v_mat[:, 1], x_real)
    return jnp.stack([y_real, y_imag], 1).reshape(k_local, 2, W * W).astype(jnp.bfloat16)


def table_kernel(reader_ref, vector_ref, degen_ref, phonon_ref, residue_ref, inverse_ref, kron_ref):
    total_r = reader_ref.shape[1]
    f32, bf16 = jnp.float32, jnp.bfloat16
    reader_id = lax.broadcasted_iota(jnp.int32, (READERS, 128), 0)
    slot_id = lax.broadcasted_iota(jnp.int32, (MOST, 128), 0)
    before = (
        lax.broadcasted_iota(jnp.int32, (128, 128), 0)
        < lax.broadcasted_iota(jnp.int32, (128, 128), 1)
    ).astype(f32).astype(bf16)
    offset = jnp.zeros((READERS, 1), f32)
    table = jnp.zeros((3 * READERS, MOST), f32)
    for block in range(total_r // 128):
        lanes = slice(block * 128, (block + 1) * 128)
        member = (reader_id == reader_ref[:, lanes]).astype(f32)
        earlier = jnp.dot(member.astype(bf16), before, preferred_element_type=f32)
        rank = jnp.sum(member * (earlier + offset), axis=0, keepdims=True)
        offset = offset + jnp.sum(member, axis=1, keepdims=True)
        place = (slot_id == rank.astype(jnp.int32)).astype(f32).astype(bf16)
        vector = vector_ref[:, lanes] + KGRID
        vector = jnp.where(vector >= KGRID, vector - KGRID, vector)
        first = vector[0:1].astype(f32)
        plane = (vector[1:2] * KGRID + vector[2:3]).astype(f32)
        degen = degen_ref[:, lanes].astype(f32)
        digits = jnp.concatenate([member * first, member * plane, member * degen], axis=0)
        table = table + lax.dot_general(
            digits.astype(bf16), place, (((1,), (1,)), ((), ())), preferred_element_type=f32
        )
    degen = table[2 * READERS :]
    used = degen > 0.5
    residue = table[:READERS] * PLANE + table[READERS : 2 * READERS]
    residue_ref[...] = jnp.where(used, residue, -1.0).astype(jnp.int32)
    inverse_ref[...] = jnp.where(used, 1.0 / jnp.where(used, degen, 1.0), 0.0)

    rows, columns = kron_ref.shape
    row = lax.broadcasted_iota(jnp.int32, (rows, columns), 0)
    column = lax.broadcasted_iota(jnp.int32, (rows, columns), 1)
    pick = lax.broadcasted_iota(jnp.int32, (rows, 32), 0) >> 4
    pick = (pick == lax.broadcasted_iota(jnp.int32, (rows, 32), 1)).astype(f32).astype(bf16)
    phonon = jnp.dot(pick, phonon_ref[...].astype(f32).astype(bf16), preferred_element_type=f32)
    point = lax.broadcasted_iota(jnp.int32, (1, columns), 1) >> 4
    second = (point >= 6).astype(jnp.int32) + (point >= 12).astype(jnp.int32)
    third = point - 6 * second
    inner = phonon[:, 1:2] * second.astype(f32) + phonon[:, 2:3] * third.astype(f32)
    inner = inner - 6.0 * jnp.floor((inner + 0.5) * (1.0 / 6.0))
    half = jnp.float32(0.5)
    root = jnp.float32(0.8671875)
    cosine = jnp.where(inner > 3.5, inner - 6.0, inner)
    cosine = jnp.abs(cosine)
    cosine = jnp.where(
        cosine < 1.5,
        jnp.where(cosine < 0.5, 1.0, half),
        jnp.where(cosine < 2.5, -half, -1.0),
    )
    sine = jnp.where(inner > 3.5, -root, root)
    sine = jnp.where((inner < 0.5) | (jnp.abs(inner - 3.0) < 0.5), 0.0, sine)
    row_part = (row >> 3) & 1
    column_part = (column >> 3) & 1
    value = jnp.where(
        row_part == column_part, cosine, jnp.where(row_part == 0, sine, -sine)
    )
    kron_ref[...] = jnp.where((row & 7) == (column & 7), value, 0.0).astype(bf16)


def k_kernel(x_ref, plane_ref, residue_ref, out_ref, z_ref, y_ref, t_ref):
    f32, bf16 = jnp.float32, jnp.bfloat16
    width = x_ref.shape[2]
    scale = (KGRID**3) ** (-0.5)
    y_ref[...] = jnp.zeros_like(y_ref)
    for k in range(KGRID):
        z_ref[k] = jnp.dot(plane_ref[...], x_ref[k], preferred_element_type=f32)

    for tile in range(PLANE // 8):
        at = tile * 8
        real = [z_ref[k, at : at + 8, :] * scale for k in range(KGRID)]
        turned = [z_ref[k, PLANE + at : PLANE + at + 8, :] * scale for k in range(KGRID)]
        for r in range(KGRID):
            total = None
            for k in range(KGRID):
                angle = 2.0 * math.pi * ((r * k) % KGRID) / KGRID
                for weight, term in ((math.cos(angle), real[k]), (math.sin(angle), turned[k])):
                    if abs(weight) < 1e-9:
                        continue
                    term = term if abs(weight - 1.0) < 1e-9 else term * weight
                    total = term if total is None else total + term
            y_ref[r * PLANE + at : r * PLANE + at + 8, 0:width] = total
    t_ref[...] = y_ref[...].T.astype(bf16)

    row_id = lax.broadcasted_iota(jnp.int32, (ROWS, 256), 0)

    def pick(step, carry):
        left = residue_ref[pl.ds(2 * step, 1), :]
        right = residue_ref[pl.ds(2 * step + 1, 1), :]
        wanted = jnp.concatenate([left, right], axis=1)
        chosen = (row_id == wanted).astype(f32).astype(bf16)
        found = jnp.dot(t_ref[...], chosen, preferred_element_type=f32)[:width].astype(bf16)
        out_ref[pl.ds(2 * step, 1)] = found[None, :, :128]
        out_ref[pl.ds(2 * step + 1, 1)] = found[None, :, 128:]
        return carry

    lax.fori_loop(0, READERS // 2, pick, 0)


def q_kernel(groups, w_ref, kron_ref, inverse_ref, out_ref, s_ref):
    f32, bf16 = jnp.float32, jnp.bfloat16
    step = pl.program_id(0)

    @pl.when(step == 0)
    def _():
        pairs = w_ref.shape[1] // 2
        used = 2 * pairs
        s_ref[:, used - used % 8 :, :] = jnp.zeros((32, s_ref.shape[1] - used + used % 8, 128), f32)
        for source in range(32):
            point, half = source // 2, source % 2
            block = w_ref[source].astype(f32)
            for part in range(2):
                s_ref[2 * point + part, half * pairs : (half + 1) * pairs, :] = block[
                    part * pairs : (part + 1) * pairs
                ]

    inverse = inverse_ref[...] * 0.25
    for group in range(groups):
        at = pl.multiple_of((step * groups + group) * 8, 8)
        data = s_ref[:, pl.ds(at, 8), :].reshape(256, 128).astype(bf16)
        found = jnp.dot(kron_ref[...], data, preferred_element_type=f32) * inverse
        out_ref[:, group * 8 : group * 8 + 8, :] = found.reshape(64, 8, 128)


def per_device(coupling, rot_k, rot_kq, r_elec, degen, reader, r_phon):
    f32, bf16 = jnp.float32, jnp.bfloat16
    k_local = coupling.shape[1]
    total_r = r_elec.shape[0]
    shape = jax.ShapeDtypeStruct
    residue, inverse, kron = pl.pallas_call(
        table_kernel,
        out_shape=(
            shape((READERS, MOST), jnp.int32),
            shape((READERS, MOST), f32),
            shape((512, 256), bf16),
        ),
        in_specs=[VMEM] * 4,
        out_specs=(VMEM,) * 3,
        cost_estimate=pl.CostEstimate(flops=10**8, bytes_accessed=10**6, transcendentals=0),
        name="tables",
    )(reader.reshape(1, total_r), r_elec.T, degen.reshape(1, total_r), r_phon)
    my_inverse = lax.dynamic_slice_in_dim(inverse, lax.axis_index("ka"), 1)

    rotated = rotate(coupling, rot_k, rot_kq)
    pieces = rotated.reshape(k_local, 2, 16, 2, 50).transpose(2, 3, 0, 1, 4)
    pieces = pieces.reshape(16, 2, k_local, 100)
    pieces = lax.all_to_all(pieces, "pb", 0, 0, tiled=True)
    pieces = lax.all_to_all(pieces.reshape(32, k_local, 100), "ka", 0, 0, tiled=True)
    x = pieces.reshape(KGRID, PLANE, 100)
    turned = jnp.concatenate([x[:, :, 50:], -x[:, :, :50]], axis=2)
    x = jnp.concatenate([x, turned], axis=1)
    slots = pl.pallas_call(
        k_kernel,
        out_shape=shape((READERS, 100, MOST), bf16),
        in_specs=[VMEM] * 3,
        out_specs=VMEM,
        scratch_shapes=[
            pltpu.VMEM((KGRID, 2 * PLANE, 100), f32),
            pltpu.VMEM((ROWS, 128), f32),
            pltpu.VMEM((128, ROWS), bf16),
        ],
        compiler_params=pltpu.CompilerParams(vmem_limit_bytes=40 * 2**20),
        name="k_transform",
    )(x, jnp.asarray(plane_table()), residue)
    w = lax.all_to_all(slots, "ka", 0, 0, tiled=True)
    groups = 3
    out = pl.pallas_call(
        lambda *refs: q_kernel(groups, *refs),
        grid=(5,),
        out_shape=shape((64, 100, MOST), f32),
        in_specs=[
            pl.BlockSpec((32, 100, MOST), lambda i: (0, 0, 0)),
            pl.BlockSpec((512, 256), lambda i: (0, 0)),
            pl.BlockSpec((1, MOST), lambda i: (0, 0)),
        ],
        out_specs=pl.BlockSpec((64, 8 * groups, MOST), lambda i: (0, i, 0)),
        scratch_shapes=[pltpu.VMEM((32, 120, MOST), f32)],
        compiler_params=pltpu.CompilerParams(
            dimension_semantics=("arbitrary",), vmem_limit_bytes=40 * 2**20
        ),
        name="q_transform",
    )(w, kron, my_inverse)
    return out.reshape(32, 2, 100, MOST)


def solution(mesh):
    in_specs = (
        P("pb", "ka", None, None),
        P("ka", None, None),
        P("pb", "ka", None, None),
        P(),
        P(),
        P(),
        P(),
    )
    out_specs = P(None, None, "pb", "ka")
    return jax.shard_map(
        per_device, mesh=mesh, in_specs=in_specs, out_specs=out_specs, check_vma=False
    )
```

```python
import math

import jax
import jax.numpy as jnp
import numpy as np
from jax import lax
from jax.experimental import pallas as pl
from jax.experimental.pallas import tpu as pltpu
from jax.sharding import PartitionSpec as P

W = 40
KGRID = 12
QGRID = 6
READERS = 32
MOST = 128
PLANE = KGRID * KGRID
ROWS = 1792
VMEM = pl.BlockSpec(memory_space=pltpu.VMEM)


def plane_table():
    index = np.arange(PLANE)
    inner = np.outer(index // KGRID, index // KGRID) + np.outer(index % KGRID, index % KGRID)
    angle = (inner % KGRID) * (2.0 * math.pi / KGRID)
    cosine, sine = np.cos(angle), np.sin(angle)
    return np.block([[cosine, sine], [-sine, cosine]]).astype(np.float32).astype(jnp.bfloat16)


def product(spec, left, right):
    return jnp.einsum(spec, left, right, preferred_element_type=jnp.float32)


def rotate(coupling, rot_k, rot_kq):
    k_local = coupling.shape[1]
    g_mat = coupling.reshape(k_local, 2, W, W)
    u_mat = rot_k.reshape(k_local, 2, W, W)
    v_mat = rot_kq.reshape(k_local, 2, W, W)
    spec = "kab,kbn->kan"
    x_real = product(spec, g_mat[:, 0], u_mat[:, 0]) - product(spec, g_mat[:, 1], u_mat[:, 1])
    x_imag = product(spec, g_mat[:, 0], u_mat[:, 1]) + product(spec, g_mat[:, 1], u_mat[:, 0])
    x_real = x_real.astype(jnp.bfloat16)
    x_imag = x_imag.astype(jnp.bfloat16)
    spec_two = "kam,kan->kmn"
    y_real = product(spec_two, v_mat[:, 0], x_real) + product(spec_two, v_mat[:, 1], x_imag)
    y_imag = product(spec_two, v_mat[:, 0], x_imag) - product(spec_two, v_mat[:, 1], x_real)
    return jnp.stack([y_real, y_imag], 1).reshape(k_local, 2, W * W).astype(jnp.bfloat16)


def table_kernel(reader_ref, vector_ref, degen_ref, phonon_ref, residue_ref, inverse_ref, kron_ref):
    total_r = reader_ref.shape[1]
    f32, bf16 = jnp.float32, jnp.bfloat16
    reader_id = lax.broadcasted_iota(jnp.int32, (READERS, 128), 0)
    slot_id = lax.broadcasted_iota(jnp.int32, (MOST, 128), 0)
    before = (
        lax.broadcasted_iota(jnp.int32, (128, 128), 0)
        < lax.broadcasted_iota(jnp.int32, (128, 128), 1)
    ).astype(f32).astype(bf16)
    offset = jnp.zeros((READERS, 1), f32)
    table = jnp.zeros((3 * READERS, MOST), f32)
    for block in range(total_r // 128):
        lanes = slice(block * 128, (block + 1) * 128)
        member = (reader_id == reader_ref[:, lanes]).astype(f32)
        earlier = jnp.dot(member.astype(bf16), before, preferred_element_type=f32)
        rank = jnp.sum(member * (earlier + offset), axis=0, keepdims=True)
        offset = offset + jnp.sum(member, axis=1, keepdims=True)
        place = (slot_id == rank.astype(jnp.int32)).astype(f32).astype(bf16)
        vector = vector_ref[:, lanes] + KGRID
        vector = jnp.where(vector >= KGRID, vector - KGRID, vector)
        first = vector[0:1].astype(f32)
        plane = (vector[1:2] * KGRID + vector[2:3]).astype(f32)
        degen = degen_ref[:, lanes].astype(f32)
        digits = jnp.concatenate([member * first, member * plane, member * degen], axis=0)
        table = table + lax.dot_general(
            digits.astype(bf16), place, (((1,), (1,)), ((), ())), preferred_element_type=f32
        )
    degen = table[2 * READERS :]
    used = degen > 0.5
    residue = table[:READERS] * PLANE + table[READERS : 2 * READERS]
    residue_ref[...] = jnp.where(used, residue, -1.0).astype(jnp.int32)
    inverse_ref[...] = jnp.where(used, 1.0 / jnp.where(used, degen, 1.0), 0.0)

    rows, columns = kron_ref.shape
    row = lax.broadcasted_iota(jnp.int32, (rows, columns), 0)
    column = lax.broadcasted_iota(jnp.int32, (rows, columns), 1)
    pick = lax.broadcasted_iota(jnp.int32, (rows, 32), 0) >> 4
    pick = (pick == lax.broadcasted_iota(jnp.int32, (rows, 32), 1)).astype(f32).astype(bf16)
    phonon = jnp.dot(pick, phonon_ref[...].astype(f32).astype(bf16), preferred_element_type=f32)
    point = lax.broadcasted_iota(jnp.int32, (1, columns), 1) >> 4
    second = (point >= 6).astype(jnp.int32) + (point >= 12).astype(jnp.int32)
    third = point - 6 * second
    inner = phonon[:, 1:2] * second.astype(f32) + phonon[:, 2:3] * third.astype(f32)
    inner = inner - 6.0 * jnp.floor((inner + 0.5) * (1.0 / 6.0))
    half = jnp.float32(0.5)
    root = jnp.float32(0.8671875)
    cosine = jnp.where(inner > 3.5, inner - 6.0, inner)
    cosine = jnp.abs(cosine)
    cosine = jnp.where(
        cosine < 1.5,
        jnp.where(cosine < 0.5, 1.0, half),
        jnp.where(cosine < 2.5, -half, -1.0),
    )
    sine = jnp.where(inner > 3.5, -root, root)
    sine = jnp.where((inner < 0.5) | (jnp.abs(inner - 3.0) < 0.5), 0.0, sine)
    row_part = row & 1
    column_part = (column >> 3) & 1
    value = jnp.where(
        row_part == column_part, cosine, jnp.where(row_part == 0, sine, -sine)
    )
    kron_ref[...] = jnp.where(((row >> 1) & 7) == (column & 7), value, 0.0).astype(bf16)


def k_kernel(x_ref, plane_ref, residue_ref, out_ref, z_ref, y_ref, t_ref):
    f32, bf16 = jnp.float32, jnp.bfloat16
    width = x_ref.shape[2]
    scale = (KGRID**3) ** (-0.5)
    y_ref[...] = jnp.zeros_like(y_ref)
    for k in range(KGRID):
        z_ref[k] = jnp.dot(plane_ref[...], x_ref[k], preferred_element_type=f32)

    for tile in range(PLANE // 8):
        at = tile * 8
        real = [z_ref[k, at : at + 8, :] * scale for k in range(KGRID)]
        turned = [z_ref[k, PLANE + at : PLANE + at + 8, :] * scale for k in range(KGRID)]
        for r in range(KGRID):
            total = None
            for k in range(KGRID):
                angle = 2.0 * math.pi * ((r * k) % KGRID) / KGRID
                for weight, term in ((math.cos(angle), real[k]), (math.sin(angle), turned[k])):
                    if abs(weight) < 1e-9:
                        continue
                    term = term if abs(weight - 1.0) < 1e-9 else term * weight
                    total = term if total is None else total + term
            y_ref[r * PLANE + at : r * PLANE + at + 8, 0:width] = total
    t_ref[...] = y_ref[...].T.astype(bf16)

    row_id = lax.broadcasted_iota(jnp.int32, (ROWS, 256), 0)

    def pick(step, carry):
        left = residue_ref[pl.ds(2 * step, 1), :]
        right = residue_ref[pl.ds(2 * step + 1, 1), :]
        wanted = jnp.concatenate([left, right], axis=1)
        chosen = (row_id == wanted).astype(f32).astype(bf16)
        found = jnp.dot(t_ref[...], chosen, preferred_element_type=f32)[:112].astype(bf16)
        out_ref[pl.ds(2 * step, 1)] = found[None, :, :128]
        out_ref[pl.ds(2 * step + 1, 1)] = found[None, :, 128:]
        return carry

    lax.fori_loop(0, READERS // 2, pick, 0)


def exchange_kernel(rotated, x_ref, out_ref, send_sem, recv_sem, self_sem):
    pb, ka = lax.axis_index("pb"), lax.axis_index("ka")
    source = lax.rem(ka // 2 + 16 - pb, 16) if rotated else pb

    def target(step):
        if not rotated:
            to = lax.rem(ka + step, 32)
            return to, pb, to
        to = lax.rem(pb + step // 2, 16)
        half = step % 2
        return 2 * to + half, to, lax.rem(2 * (pb + to) + half, 32)

    def is_self(to_pb, to_ka):
        return jnp.logical_and(to_pb == pb, to_ka == ka)

    def remote(step, row, landing, device):
        return pltpu.make_async_remote_copy(
            src_ref=x_ref.at[row],
            dst_ref=out_ref.at[landing],
            send_sem=send_sem.at[step],
            recv_sem=recv_sem.at[landing],
            device_id=device,
            device_id_type=pl.DeviceIdType.MESH,
        )

    barrier = pltpu.get_barrier_semaphore()

    def greet(other, carry):
        @pl.when(jnp.logical_not(is_self(source, other)))
        def _():
            pl.semaphore_signal(
                barrier, inc=1, device_id=(source, other), device_id_type=pl.DeviceIdType.MESH
            )

        return carry

    lax.fori_loop(0, 32, greet, 0)
    pl.semaphore_wait(barrier, 31 if not rotated else jnp.where(source == pb, 31, 32))

    def send(step, carry):
        row, to_pb, to_ka = target(step)
        own = is_self(to_pb, to_ka)

        @pl.when(own)
        def _():
            pltpu.make_async_copy(x_ref.at[row], out_ref.at[ka], self_sem).start()

        @pl.when(jnp.logical_not(own))
        def _():
            remote(step, row, ka, (to_pb, to_ka)).start()

        return carry

    lax.fori_loop(0, 32, send, 0)

    def receive(other, carry):
        own = is_self(source, other)

        @pl.when(own)
        def _():
            pltpu.make_async_copy(x_ref.at[0], out_ref.at[other], self_sem).wait()

        @pl.when(jnp.logical_not(own))
        def _():
            remote(0, 0, other, (source, other)).wait_recv()

        return carry

    lax.fori_loop(0, 32, receive, 0)

    def sent(step, carry):
        row, to_pb, to_ka = target(step)

        @pl.when(jnp.logical_not(is_self(to_pb, to_ka)))
        def _():
            remote(step, row, ka, (to_pb, to_ka)).wait_send()

        return carry

    lax.fori_loop(0, 32, sent, 0)


def exchange(x, rotated, number, name):
    return pl.pallas_call(
        lambda *refs: exchange_kernel(rotated, *refs),
        out_shape=jax.ShapeDtypeStruct(x.shape, x.dtype),
        in_specs=[VMEM],
        out_specs=VMEM,
        scratch_shapes=[
            pltpu.SemaphoreType.DMA((32,)),
            pltpu.SemaphoreType.DMA((32,)),
            pltpu.SemaphoreType.DMA,
        ],
        compiler_params=pltpu.CompilerParams(collective_id=number, has_side_effects=True),
        name=name,
    )(x)


def q_kernel(groups, w_ref, kron_ref, inverse_ref, out_ref, s_ref):
    f32, bf16 = jnp.float32, jnp.bfloat16
    step = pl.program_id(0)

    @pl.when(step == 0)
    def _():
        pairs = 50
        shift = 2 * lax.axis_index("pb")
        used = 2 * pairs
        s_ref[:, used - used % 8 :, :] = jnp.zeros((32, s_ref.shape[1] - used + used % 8, 128), f32)
        for source in range(32):
            point, half = source // 2, source % 2
            block = w_ref[lax.rem(source + shift, 32)].astype(f32)
            for part in range(2):
                s_ref[2 * point + part, half * pairs : (half + 1) * pairs, :] = block[
                    part * pairs : (part + 1) * pairs
                ]

    inverse = inverse_ref[...] * 0.25
    for group in range(groups):
        at = pl.multiple_of((step * groups + group) * 8, 8)
        data = s_ref[:, pl.ds(at, 8), :].reshape(256, 128).astype(bf16)
        found = jnp.dot(kron_ref[...], data, preferred_element_type=f32) * inverse
        out_ref[:, group * 16 : group * 16 + 16, :] = found.reshape(32, 16, 128)


def per_device(coupling, rot_k, rot_kq, r_elec, degen, reader, r_phon):
    f32, bf16 = jnp.float32, jnp.bfloat16
    k_local = coupling.shape[1]
    total_r = r_elec.shape[0]
    shape = jax.ShapeDtypeStruct
    residue, inverse, kron = pl.pallas_call(
        table_kernel,
        out_shape=(
            shape((READERS, MOST), jnp.int32),
            shape((READERS, MOST), f32),
            shape((512, 256), bf16),
        ),
        in_specs=[VMEM] * 4,
        out_specs=(VMEM,) * 3,
        cost_estimate=pl.CostEstimate(flops=10**8, bytes_accessed=10**6, transcendentals=0),
        name="tables",
    )(reader.reshape(1, total_r), r_elec.T, degen.reshape(1, total_r), r_phon)
    my_inverse = lax.dynamic_slice_in_dim(inverse, lax.axis_index("ka"), 1)

    rotated = rotate(coupling, rot_k, rot_kq)
    pieces = rotated.reshape(k_local, 2, 16, 2, 50).transpose(2, 3, 0, 1, 4)
    pieces = pieces.reshape(32, k_local, 100)
    pieces = jnp.pad(pieces, ((0, 0), (0, 64 - k_local), (0, 28)))
    pieces = exchange(pieces, True, 1, "to_pairs")[:, :k_local, :100]
    x = pieces.reshape(KGRID, PLANE, 100)
    turned = jnp.concatenate([x[:, :, 50:], -x[:, :, :50]], axis=2)
    x = jnp.concatenate([x, turned], axis=1)
    slots = pl.pallas_call(
        k_kernel,
        out_shape=shape((READERS, 112, MOST), bf16),
        in_specs=[VMEM] * 3,
        out_specs=VMEM,
        scratch_shapes=[
            pltpu.VMEM((KGRID, 2 * PLANE, 100), f32),
            pltpu.VMEM((ROWS, 128), f32),
            pltpu.VMEM((128, ROWS), bf16),
        ],
        compiler_params=pltpu.CompilerParams(vmem_limit_bytes=40 * 2**20),
        name="k_transform",
    )(x, jnp.asarray(plane_table()), residue)
    w = exchange(slots, False, 2, "to_readers")
    groups = 3
    out = pl.pallas_call(
        lambda *refs: q_kernel(groups, *refs),
        grid=(5,),
        out_shape=shape((32, 200, MOST), f32),
        in_specs=[
            pl.BlockSpec((32, 112, MOST), lambda i: (0, 0, 0)),
            pl.BlockSpec((512, 256), lambda i: (0, 0)),
            pl.BlockSpec((1, MOST), lambda i: (0, 0)),
        ],
        out_specs=pl.BlockSpec((32, 16 * groups, MOST), lambda i: (0, i, 0)),
        scratch_shapes=[pltpu.VMEM((32, 120, MOST), f32)],
        compiler_params=pltpu.CompilerParams(
            dimension_semantics=("arbitrary",), vmem_limit_bytes=40 * 2**20
        ),
        name="q_transform",
    )(w, kron, my_inverse)
    return out.reshape(32, 100, 2, MOST).transpose(0, 2, 1, 3)


def solution(mesh):
    in_specs = (
        P("pb", "ka", None, None),
        P("ka", None, None),
        P("pb", "ka", None, None),
        P(),
        P(),
        P(),
        P(),
    )
    out_specs = P(None, None, "pb", "ka")
    return jax.shard_map(
        per_device, mesh=mesh, in_specs=in_specs, out_specs=out_specs, check_vma=False
    )
```

```python
import math

import jax
import jax.numpy as jnp
import numpy as np
from jax import lax
from jax.experimental import pallas as pl
from jax.experimental.pallas import tpu as pltpu
from jax.sharding import PartitionSpec as P

W = 40
KGRID = 12
QGRID = 6
READERS = 32
MOST = 128
PLANE = KGRID * KGRID
ROWS = 1792
VMEM = pl.BlockSpec(memory_space=pltpu.VMEM)


def plane_table():
    index = np.arange(PLANE)
    inner = np.outer(index // KGRID, index // KGRID) + np.outer(index % KGRID, index % KGRID)
    angle = (inner % KGRID) * (2.0 * math.pi / KGRID)
    cosine, sine = np.cos(angle), np.sin(angle)
    return np.block([[cosine, sine], [-sine, cosine]]).astype(np.float32).astype(jnp.bfloat16)


def product(spec, left, right):
    return jnp.einsum(spec, left, right, preferred_element_type=jnp.float32)


def rotate(coupling, rot_k, rot_kq):
    k_local = coupling.shape[1]
    g_mat = coupling.reshape(k_local, 2, W, W)
    u_mat = rot_k.reshape(k_local, 2, W, W)
    v_mat = rot_kq.reshape(k_local, 2, W, W)
    spec = "kab,kbn->kan"
    x_real = product(spec, g_mat[:, 0], u_mat[:, 0]) - product(spec, g_mat[:, 1], u_mat[:, 1])
    x_imag = product(spec, g_mat[:, 0], u_mat[:, 1]) + product(spec, g_mat[:, 1], u_mat[:, 0])
    x_real = x_real.astype(jnp.bfloat16)
    x_imag = x_imag.astype(jnp.bfloat16)
    spec_two = "kam,kan->kmn"
    y_real = product(spec_two, v_mat[:, 0], x_real) + product(spec_two, v_mat[:, 1], x_imag)
    y_imag = product(spec_two, v_mat[:, 0], x_imag) - product(spec_two, v_mat[:, 1], x_real)
    return jnp.stack([y_real, y_imag], 1).reshape(k_local, 2, W * W).astype(jnp.bfloat16)


def table_kernel(reader_ref, vector_ref, degen_ref, phonon_ref, residue_ref, inverse_ref, kron_ref):
    total_r = reader_ref.shape[1]
    f32, bf16 = jnp.float32, jnp.bfloat16
    reader_id = lax.broadcasted_iota(jnp.int32, (READERS, 128), 0)
    slot_id = lax.broadcasted_iota(jnp.int32, (MOST, 128), 0)
    before = (
        lax.broadcasted_iota(jnp.int32, (128, 128), 0)
        < lax.broadcasted_iota(jnp.int32, (128, 128), 1)
    ).astype(f32).astype(bf16)
    offset = jnp.zeros((READERS, 1), f32)
    table = jnp.zeros((3 * READERS, MOST), f32)
    for block in range(total_r // 128):
        lanes = slice(block * 128, (block + 1) * 128)
        member = (reader_id == reader_ref[:, lanes]).astype(f32)
        earlier = jnp.dot(member.astype(bf16), before, preferred_element_type=f32)
        rank = jnp.sum(member * (earlier + offset), axis=0, keepdims=True)
        offset = offset + jnp.sum(member, axis=1, keepdims=True)
        place = (slot_id == rank.astype(jnp.int32)).astype(f32).astype(bf16)
        vector = vector_ref[:, lanes] + KGRID
        vector = jnp.where(vector >= KGRID, vector - KGRID, vector)
        first = vector[0:1].astype(f32)
        plane = (vector[1:2] * KGRID + vector[2:3]).astype(f32)
        degen = degen_ref[:, lanes].astype(f32)
        digits = jnp.concatenate([member * first, member * plane, member * degen], axis=0)
        table = table + lax.dot_general(
            digits.astype(bf16), place, (((1,), (1,)), ((), ())), preferred_element_type=f32
        )
    degen = table[2 * READERS :]
    used = degen > 0.5
    residue = table[:READERS] * PLANE + table[READERS : 2 * READERS]
    residue_ref[...] = jnp.where(used, residue, -1.0).astype(jnp.int32)
    inverse_ref[...] = jnp.where(used, 1.0 / jnp.where(used, degen, 1.0), 0.0)

    rows, columns = kron_ref.shape
    row = lax.broadcasted_iota(jnp.int32, (rows, columns), 0)
    column = lax.broadcasted_iota(jnp.int32, (rows, columns), 1)
    pick = lax.broadcasted_iota(jnp.int32, (rows, 32), 0) >> 4
    pick = (pick == lax.broadcasted_iota(jnp.int32, (rows, 32), 1)).astype(f32).astype(bf16)
    phonon = jnp.dot(pick, phonon_ref[...].astype(f32).astype(bf16), preferred_element_type=f32)
    point = lax.broadcasted_iota(jnp.int32, (1, columns), 1) >> 4
    second = (point >= 6).astype(jnp.int32) + (point >= 12).astype(jnp.int32)
    third = point - 6 * second
    inner = phonon[:, 1:2] * second.astype(f32) + phonon[:, 2:3] * third.astype(f32)
    inner = inner - 6.0 * jnp.floor((inner + 0.5) * (1.0 / 6.0))
    half = jnp.float32(0.5)
    root = jnp.float32(0.8671875)
    cosine = jnp.where(inner > 3.5, inner - 6.0, inner)
    cosine = jnp.abs(cosine)
    cosine = jnp.where(
        cosine < 1.5,
        jnp.where(cosine < 0.5, 1.0, half),
        jnp.where(cosine < 2.5, -half, -1.0),
    )
    sine = jnp.where(inner > 3.5, -root, root)
    sine = jnp.where((inner < 0.5) | (jnp.abs(inner - 3.0) < 0.5), 0.0, sine)
    row_part = row & 1
    column_part = (column >> 3) & 1
    value = jnp.where(
        row_part == column_part, cosine, jnp.where(row_part == 0, sine, -sine)
    )
    kron_ref[...] = jnp.where(((row >> 1) & 7) == (column & 7), value, 0.0).astype(bf16)


def k_kernel(x_ref, plane_ref, residue_ref, out_ref, z_ref, y_ref, t_ref):
    f32, bf16 = jnp.float32, jnp.bfloat16
    width = x_ref.shape[2]
    scale = (KGRID**3) ** (-0.5)
    y_ref[...] = jnp.zeros_like(y_ref)
    for k in range(KGRID):
        z_ref[k] = jnp.dot(plane_ref[...], x_ref[k], preferred_element_type=f32)

    for tile in range(PLANE // 8):
        at = tile * 8
        real = [z_ref[k, at : at + 8, :] * scale for k in range(KGRID)]
        turned = [z_ref[k, PLANE + at : PLANE + at + 8, :] * scale for k in range(KGRID)]
        for r in range(KGRID):
            total = None
            for k in range(KGRID):
                angle = 2.0 * math.pi * ((r * k) % KGRID) / KGRID
                for weight, term in ((math.cos(angle), real[k]), (math.sin(angle), turned[k])):
                    if abs(weight) < 1e-9:
                        continue
                    term = term if abs(weight - 1.0) < 1e-9 else term * weight
                    total = term if total is None else total + term
            y_ref[r * PLANE + at : r * PLANE + at + 8, 0:width] = total
    t_ref[...] = y_ref[...].T.astype(bf16)

    row_id = lax.broadcasted_iota(jnp.int32, (ROWS, 256), 0)

    def pick(step, carry):
        left = residue_ref[pl.ds(2 * step, 1), :]
        right = residue_ref[pl.ds(2 * step + 1, 1), :]
        wanted = jnp.concatenate([left, right], axis=1)
        chosen = (row_id == wanted).astype(f32).astype(bf16)
        found = jnp.dot(t_ref[...], chosen, preferred_element_type=f32)[:104].astype(bf16)
        out_ref[pl.ds(2 * step, 1)] = found[None, :, :128]
        out_ref[pl.ds(2 * step + 1, 1)] = found[None, :, 128:]
        return carry

    lax.fori_loop(0, READERS // 2, pick, 0)


def exchange_kernel(rotated, x_ref, out_ref, send_sem, recv_sem, self_sem):
    pb, ka = lax.axis_index("pb"), lax.axis_index("ka")
    source = lax.rem(ka // 2 + 16 - pb, 16) if rotated else pb

    def target(step):
        if not rotated:
            shift = lax.rem(13 * step, 32)
            to = lax.rem(ka // 8 + shift // 8, 4) * 8 + lax.rem(ka + shift, 8)
            return to, pb, to
        to = lax.rem(pb + 5 * (step // 2), 16)
        half = step % 2
        return 2 * to + half, to, lax.rem(2 * (pb + to) + half, 32)

    def is_self(to_pb, to_ka):
        return jnp.logical_and(to_pb == pb, to_ka == ka)

    def remote(step, row, landing, device):
        return pltpu.make_async_remote_copy(
            src_ref=x_ref.at[row],
            dst_ref=out_ref.at[landing],
            send_sem=send_sem.at[step],
            recv_sem=recv_sem.at[landing],
            device_id=device,
            device_id_type=pl.DeviceIdType.MESH,
        )

    barrier = pltpu.get_barrier_semaphore()

    def greet(other, carry):
        @pl.when(jnp.logical_not(is_self(source, other)))
        def _():
            pl.semaphore_signal(
                barrier, inc=1, device_id=(source, other), device_id_type=pl.DeviceIdType.MESH
            )

        return carry

    lax.fori_loop(0, 32, greet, 0)
    pl.semaphore_wait(barrier, 31 if not rotated else jnp.where(source == pb, 31, 32))

    def send(step, carry):
        row, to_pb, to_ka = target(step)
        own = is_self(to_pb, to_ka)

        @pl.when(own)
        def _():
            pltpu.make_async_copy(x_ref.at[row], out_ref.at[ka], self_sem).start()

        @pl.when(jnp.logical_not(own))
        def _():
            remote(step, row, ka, (to_pb, to_ka)).start()

        return carry

    lax.fori_loop(0, 32, send, 0)

    def receive(other, carry):
        own = is_self(source, other)

        @pl.when(own)
        def _():
            pltpu.make_async_copy(x_ref.at[0], out_ref.at[other], self_sem).wait()

        @pl.when(jnp.logical_not(own))
        def _():
            remote(0, 0, other, (source, other)).wait_recv()

        return carry

    lax.fori_loop(0, 32, receive, 0)

    def sent(step, carry):
        row, to_pb, to_ka = target(step)

        @pl.when(jnp.logical_not(is_self(to_pb, to_ka)))
        def _():
            remote(step, row, ka, (to_pb, to_ka)).wait_send()

        return carry

    lax.fori_loop(0, 32, sent, 0)


def exchange(x, rotated, number, name):
    return pl.pallas_call(
        lambda *refs: exchange_kernel(rotated, *refs),
        out_shape=jax.ShapeDtypeStruct(x.shape, x.dtype),
        in_specs=[VMEM],
        out_specs=VMEM,
        scratch_shapes=[
            pltpu.SemaphoreType.DMA((32,)),
            pltpu.SemaphoreType.DMA((32,)),
            pltpu.SemaphoreType.DMA,
        ],
        compiler_params=pltpu.CompilerParams(collective_id=number, has_side_effects=True),
        name=name,
    )(x)


def q_kernel(groups, w_ref, kron_ref, inverse_ref, out_ref, s_ref):
    f32, bf16 = jnp.float32, jnp.bfloat16
    step = pl.program_id(0)

    @pl.when(step == 0)
    def _():
        pairs = 50
        shift = 2 * lax.axis_index("pb")
        used = 2 * pairs
        s_ref[:, used - used % 8 :, :] = jnp.zeros((32, s_ref.shape[1] - used + used % 8, 128), f32)
        for source in range(32):
            point, half = source // 2, source % 2
            block = w_ref[lax.rem(source + shift, 32)].astype(f32)
            for part in range(2):
                s_ref[2 * point + part, half * pairs : (half + 1) * pairs, :] = block[
                    part * pairs : (part + 1) * pairs
                ]

    inverse = inverse_ref[pl.ds(lax.axis_index("ka"), 1), :] * 0.25
    for group in range(groups):
        at = pl.multiple_of((step * groups + group) * 8, 8)
        data = s_ref[:, pl.ds(at, 8), :].reshape(256, 128).astype(bf16)
        found = jnp.dot(kron_ref[...], data, preferred_element_type=f32) * inverse
        out_ref[:, group * 16 : group * 16 + 16, :] = found.reshape(32, 16, 128)


def per_device(coupling, rot_k, rot_kq, r_elec, degen, reader, r_phon):
    f32, bf16 = jnp.float32, jnp.bfloat16
    k_local = coupling.shape[1]
    total_r = r_elec.shape[0]
    shape = jax.ShapeDtypeStruct
    residue, inverse, kron = pl.pallas_call(
        table_kernel,
        out_shape=(
            shape((READERS, MOST), jnp.int32),
            shape((READERS, MOST), f32),
            shape((512, 256), bf16),
        ),
        in_specs=[VMEM] * 4,
        out_specs=(VMEM,) * 3,
        cost_estimate=pl.CostEstimate(flops=10**8, bytes_accessed=10**6, transcendentals=0),
        name="tables",
    )(reader.reshape(1, total_r), r_elec.T, degen.reshape(1, total_r), r_phon)

    rotated = rotate(coupling, rot_k, rot_kq)
    pieces = rotated.reshape(k_local, 2, 16, 2, 50).transpose(2, 3, 0, 1, 4)
    pieces = pieces.reshape(32, k_local, 100)
    pieces = jnp.pad(pieces, ((0, 0), (0, 56 - k_local), (0, 28)))
    pieces = exchange(pieces, True, 1, "to_pairs")[:, :k_local, :100]
    x = pieces.reshape(KGRID, PLANE, 100)
    turned = jnp.concatenate([x[:, :, 50:], -x[:, :, :50]], axis=2)
    x = jnp.concatenate([x, turned], axis=1)
    slots = pl.pallas_call(
        k_kernel,
        out_shape=shape((READERS, 104, MOST), bf16),
        in_specs=[VMEM] * 3,
        out_specs=VMEM,
        scratch_shapes=[
            pltpu.VMEM((KGRID, 2 * PLANE, 100), f32),
            pltpu.VMEM((ROWS, 128), f32),
            pltpu.VMEM((128, ROWS), bf16),
        ],
        compiler_params=pltpu.CompilerParams(vmem_limit_bytes=40 * 2**20),
        name="k_transform",
    )(x, jnp.asarray(plane_table()), residue)
    w = exchange(slots, False, 2, "to_readers")
    groups = 3
    out = pl.pallas_call(
        lambda *refs: q_kernel(groups, *refs),
        grid=(5,),
        out_shape=shape((32, 200, MOST), f32),
        in_specs=[
            pl.BlockSpec((32, 104, MOST), lambda i: (0, 0, 0)),
            pl.BlockSpec((512, 256), lambda i: (0, 0)),
            pl.BlockSpec((READERS, MOST), lambda i: (0, 0)),
        ],
        out_specs=pl.BlockSpec((32, 16 * groups, MOST), lambda i: (0, i, 0)),
        scratch_shapes=[pltpu.VMEM((32, 120, MOST), f32)],
        compiler_params=pltpu.CompilerParams(
            dimension_semantics=("arbitrary",), vmem_limit_bytes=40 * 2**20
        ),
        name="q_transform",
    )(w, kron, inverse)
    return out.reshape(32, 100, 2, MOST).transpose(0, 2, 1, 3)


def solution(mesh):
    in_specs = (
        P("pb", "ka", None, None),
        P("ka", None, None),
        P("pb", "ka", None, None),
        P(),
        P(),
        P(),
        P(),
    )
    out_specs = P(None, None, "pb", "ka")
    return jax.shard_map(
        per_device, mesh=mesh, in_specs=in_specs, out_specs=out_specs, check_vma=False
    )
```

```python
import math

import jax
import jax.numpy as jnp
import numpy as np
from jax import lax
from jax.experimental import pallas as pl
from jax.experimental.pallas import tpu as pltpu
from jax.sharding import PartitionSpec as P

W = 40
KGRID = 12
QGRID = 6
READERS = 32
MOST = 128
PLANE = KGRID * KGRID
ROWS = 1792
VMEM = pl.BlockSpec(memory_space=pltpu.VMEM)


def plane_table():
    index = np.arange(PLANE)
    inner = np.outer(index // KGRID, index // KGRID) + np.outer(index % KGRID, index % KGRID)
    angle = (inner % KGRID) * (2.0 * math.pi / KGRID)
    cosine, sine = np.cos(angle), np.sin(angle)
    return np.block([[cosine, sine], [-sine, cosine]]).astype(np.float32).astype(jnp.bfloat16)


def product(spec, left, right):
    return jnp.einsum(spec, left, right, preferred_element_type=jnp.float32)


def rotate(coupling, rot_k, rot_kq):
    k_local = coupling.shape[1]
    g_mat = coupling.reshape(k_local, 2, W, W)
    u_mat = rot_k.reshape(k_local, 2, W, W)
    v_mat = rot_kq.reshape(k_local, 2, W, W)
    spec = "kab,kbn->kan"
    x_real = product(spec, g_mat[:, 0], u_mat[:, 0]) - product(spec, g_mat[:, 1], u_mat[:, 1])
    x_imag = product(spec, g_mat[:, 0], u_mat[:, 1]) + product(spec, g_mat[:, 1], u_mat[:, 0])
    x_real = x_real.astype(jnp.bfloat16)
    x_imag = x_imag.astype(jnp.bfloat16)
    spec_two = "kam,kan->kmn"
    y_real = product(spec_two, v_mat[:, 0], x_real) + product(spec_two, v_mat[:, 1], x_imag)
    y_imag = product(spec_two, v_mat[:, 0], x_imag) - product(spec_two, v_mat[:, 1], x_real)
    return jnp.stack([y_real, y_imag], 1).reshape(k_local, 2, W * W).astype(jnp.bfloat16)


def table_kernel(reader_ref, vector_ref, degen_ref, residue_ref, inverse_ref):
    total_r = reader_ref.shape[1]
    f32, bf16 = jnp.float32, jnp.bfloat16
    reader_id = lax.broadcasted_iota(jnp.int32, (READERS, 128), 0)
    slot_id = lax.broadcasted_iota(jnp.int32, (MOST, 128), 0)
    before = (
        lax.broadcasted_iota(jnp.int32, (128, 128), 0)
        < lax.broadcasted_iota(jnp.int32, (128, 128), 1)
    ).astype(f32).astype(bf16)
    offset = jnp.zeros((READERS, 1), f32)
    table = jnp.zeros((3 * READERS, MOST), f32)
    for block in range(total_r // 128):
        lanes = slice(block * 128, (block + 1) * 128)
        member = (reader_id == reader_ref[:, lanes]).astype(f32)
        earlier = jnp.dot(member.astype(bf16), before, preferred_element_type=f32)
        rank = jnp.sum(member * (earlier + offset), axis=0, keepdims=True)
        offset = offset + jnp.sum(member, axis=1, keepdims=True)
        place = (slot_id == rank.astype(jnp.int32)).astype(f32).astype(bf16)
        vector = vector_ref[:, lanes] + KGRID
        vector = jnp.where(vector >= KGRID, vector - KGRID, vector)
        first = vector[0:1].astype(f32)
        plane = (vector[1:2] * KGRID + vector[2:3]).astype(f32)
        degen = degen_ref[:, lanes].astype(f32)
        digits = jnp.concatenate([member * first, member * plane, member * degen], axis=0)
        table = table + lax.dot_general(
            digits.astype(bf16), place, (((1,), (1,)), ((), ())), preferred_element_type=f32
        )
    degen = table[2 * READERS :]
    used = degen > 0.5
    residue = table[:READERS] * PLANE + table[READERS : 2 * READERS]
    residue_ref[...] = jnp.where(used, residue, -1.0).astype(jnp.int32)
    inverse_ref[...] = jnp.where(used, 1.0 / jnp.where(used, degen, 1.0), 0.0)


def phonon_kernel(phonon_ref, kron_ref):
    f32, bf16 = jnp.float32, jnp.bfloat16
    rows, columns = kron_ref.shape
    row = lax.broadcasted_iota(jnp.int32, (rows, columns), 0)
    column = lax.broadcasted_iota(jnp.int32, (rows, columns), 1)
    pick = lax.broadcasted_iota(jnp.int32, (rows, 32), 0) >> 4
    pick = (pick == lax.broadcasted_iota(jnp.int32, (rows, 32), 1)).astype(f32).astype(bf16)
    phonon = jnp.dot(pick, phonon_ref[...].astype(f32).astype(bf16), preferred_element_type=f32)
    point = lax.broadcasted_iota(jnp.int32, (1, columns), 1) >> 4
    second = (point >= 6).astype(jnp.int32) + (point >= 12).astype(jnp.int32)
    third = point - 6 * second
    inner = phonon[:, 1:2] * second.astype(f32) + phonon[:, 2:3] * third.astype(f32)
    inner = inner - 6.0 * jnp.floor((inner + 0.5) * (1.0 / 6.0))
    half = jnp.float32(0.5)
    root = jnp.float32(0.8671875)
    cosine = jnp.where(inner > 3.5, inner - 6.0, inner)
    cosine = jnp.abs(cosine)
    cosine = jnp.where(
        cosine < 1.5,
        jnp.where(cosine < 0.5, 1.0, half),
        jnp.where(cosine < 2.5, -half, -1.0),
    )
    sine = jnp.where(inner > 3.5, -root, root)
    sine = jnp.where((inner < 0.5) | (jnp.abs(inner - 3.0) < 0.5), 0.0, sine)
    row_part = row & 1
    column_part = (column >> 3) & 1
    value = jnp.where(
        row_part == column_part, cosine, jnp.where(row_part == 0, sine, -sine)
    )
    kron_ref[...] = jnp.where(((row >> 1) & 7) == (column & 7), value, 0.0).astype(bf16)


def k_kernel(x_ref, plane_ref, residue_ref, out_ref, z_ref, y_ref, t_ref):
    f32, bf16 = jnp.float32, jnp.bfloat16
    width = x_ref.shape[2]
    scale = (KGRID**3) ** (-0.5)
    y_ref[...] = jnp.zeros_like(y_ref)
    for k in range(KGRID):
        z_ref[k] = jnp.dot(plane_ref[...], x_ref[k], preferred_element_type=f32)

    for tile in range(PLANE // 8):
        at = tile * 8
        real = [z_ref[k, at : at + 8, :] * scale for k in range(KGRID)]
        turned = [z_ref[k, PLANE + at : PLANE + at + 8, :] * scale for k in range(KGRID)]
        for r in range(KGRID):
            total = None
            for k in range(KGRID):
                angle = 2.0 * math.pi * ((r * k) % KGRID) / KGRID
                for weight, term in ((math.cos(angle), real[k]), (math.sin(angle), turned[k])):
                    if abs(weight) < 1e-9:
                        continue
                    term = term if abs(weight - 1.0) < 1e-9 else term * weight
                    total = term if total is None else total + term
            y_ref[r * PLANE + at : r * PLANE + at + 8, 0:width] = total
    t_ref[...] = y_ref[...].T.astype(bf16)

    row_id = lax.broadcasted_iota(jnp.int32, (ROWS, 256), 0)

    def pick(step, carry):
        left = residue_ref[pl.ds(2 * step, 1), :]
        right = residue_ref[pl.ds(2 * step + 1, 1), :]
        wanted = jnp.concatenate([left, right], axis=1)
        chosen = (row_id == wanted).astype(f32).astype(bf16)
        found = jnp.dot(t_ref[...], chosen, preferred_element_type=f32)[:width].astype(bf16)
        out_ref[pl.ds(2 * step, 1)] = found[None, :, :128]
        out_ref[pl.ds(2 * step + 1, 1)] = found[None, :, 128:]
        return carry

    lax.fori_loop(0, READERS // 2, pick, 0)


def exchange_kernel(x_ref, out_ref, send_sem, recv_sem, self_sem):
    pb, ka = lax.axis_index("pb"), lax.axis_index("ka")
    source = lax.rem(ka // 2 + 16 - pb, 16)

    def target(step):
        to = lax.rem(pb + 5 * (step // 2), 16)
        half = step % 2
        return 2 * to + half, to, lax.rem(2 * (pb + to) + half, 32)

    def is_self(to_pb, to_ka):
        return jnp.logical_and(to_pb == pb, to_ka == ka)

    def remote(step, row, landing, device):
        return pltpu.make_async_remote_copy(
            src_ref=x_ref.at[row],
            dst_ref=out_ref.at[landing],
            send_sem=send_sem.at[step],
            recv_sem=recv_sem.at[landing],
            device_id=device,
            device_id_type=pl.DeviceIdType.MESH,
        )

    barrier = pltpu.get_barrier_semaphore()

    def greet(other, carry):
        @pl.when(jnp.logical_not(is_self(source, other)))
        def _():
            pl.semaphore_signal(
                barrier, inc=1, device_id=(source, other), device_id_type=pl.DeviceIdType.MESH
            )

        return carry

    lax.fori_loop(0, 32, greet, 0)
    pl.semaphore_wait(barrier, jnp.where(source == pb, 31, 32))

    def send(step, carry):
        row, to_pb, to_ka = target(step)
        own = is_self(to_pb, to_ka)

        @pl.when(own)
        def _():
            pltpu.make_async_copy(x_ref.at[row], out_ref.at[ka], self_sem).start()

        @pl.when(jnp.logical_not(own))
        def _():
            remote(step, row, ka, (to_pb, to_ka)).start()

        return carry

    lax.fori_loop(0, 32, send, 0)

    def receive(other, carry):
        own = is_self(source, other)

        @pl.when(own)
        def _():
            pltpu.make_async_copy(x_ref.at[0], out_ref.at[other], self_sem).wait()

        @pl.when(jnp.logical_not(own))
        def _():
            remote(0, 0, other, (source, other)).wait_recv()

        return carry

    lax.fori_loop(0, 32, receive, 0)

    def sent(step, carry):
        row, to_pb, to_ka = target(step)

        @pl.when(jnp.logical_not(is_self(to_pb, to_ka)))
        def _():
            remote(step, row, ka, (to_pb, to_ka)).wait_send()

        return carry

    lax.fori_loop(0, 32, sent, 0)


def exchange(x, number, name):
    return pl.pallas_call(
        exchange_kernel,
        out_shape=jax.ShapeDtypeStruct(x.shape, x.dtype),
        in_specs=[VMEM],
        out_specs=VMEM,
        scratch_shapes=[
            pltpu.SemaphoreType.DMA((32,)),
            pltpu.SemaphoreType.DMA((32,)),
            pltpu.SemaphoreType.DMA,
        ],
        compiler_params=pltpu.CompilerParams(collective_id=number, has_side_effects=True),
        name=name,
    )(x)


def q_kernel(groups, w_ref, kron_ref, inverse_ref, out_ref, s_ref):
    f32, bf16 = jnp.float32, jnp.bfloat16
    step = pl.program_id(0)

    @pl.when(step == 0)
    def _():
        pairs = 50
        shift = 2 * lax.axis_index("pb")
        used = 2 * pairs
        s_ref[:, used - used % 8 :, :] = jnp.zeros((32, s_ref.shape[1] - used + used % 8, 128), f32)
        for source in range(32):
            point, half = source // 2, source % 2
            block = w_ref[lax.rem(source + shift, 32)].astype(f32)
            for part in range(2):
                s_ref[2 * point + part, half * pairs : (half + 1) * pairs, :] = block[
                    part * pairs : (part + 1) * pairs
                ]

    inverse = inverse_ref[pl.ds(lax.axis_index("ka"), 1), :] * 0.25
    for group in range(groups):
        at = pl.multiple_of((step * groups + group) * 8, 8)
        data = s_ref[:, pl.ds(at, 8), :].reshape(256, 128).astype(bf16)
        found = jnp.dot(kron_ref[...], data, preferred_element_type=f32) * inverse
        out_ref[:, group * 16 : group * 16 + 16, :] = found.reshape(32, 16, 128)


def per_device(coupling, rot_k, rot_kq, r_elec, degen, reader, r_phon):
    f32, bf16 = jnp.float32, jnp.bfloat16
    k_local = coupling.shape[1]
    total_r = r_elec.shape[0]
    shape = jax.ShapeDtypeStruct
    residue, inverse = pl.pallas_call(
        table_kernel,
        out_shape=(
            shape((READERS, MOST), jnp.int32),
            shape((READERS, MOST), f32),
        ),
        in_specs=[VMEM] * 3,
        out_specs=(VMEM,) * 2,
        cost_estimate=pl.CostEstimate(flops=10**8, bytes_accessed=10**6, transcendentals=0),
        name="tables",
    )(reader.reshape(1, total_r), r_elec.T, degen.reshape(1, total_r))
    kron = pl.pallas_call(
        phonon_kernel,
        out_shape=shape((512, 256), bf16),
        in_specs=[VMEM],
        out_specs=VMEM,
        cost_estimate=pl.CostEstimate(flops=10**8, bytes_accessed=10**6, transcendentals=0),
        name="phonon_table",
    )(r_phon)

    rotated = rotate(coupling, rot_k, rot_kq)
    pieces = rotated.reshape(k_local, 2, 16, 2, 50).transpose(2, 3, 0, 1, 4)
    pieces = pieces.reshape(32, k_local, 100)
    pieces = jnp.pad(pieces, ((0, 0), (0, 56 - k_local), (0, 28)))
    pieces = exchange(pieces, 1, "to_pairs")[:, :k_local, :100]
    x = pieces.reshape(KGRID, PLANE, 100)
    turned = jnp.concatenate([x[:, :, 50:], -x[:, :, :50]], axis=2)
    x = jnp.concatenate([x, turned], axis=1)
    slots = pl.pallas_call(
        k_kernel,
        out_shape=shape((READERS, 100, MOST), bf16),
        in_specs=[VMEM] * 3,
        out_specs=VMEM,
        scratch_shapes=[
            pltpu.VMEM((KGRID, 2 * PLANE, 100), f32),
            pltpu.VMEM((ROWS, 128), f32),
            pltpu.VMEM((128, ROWS), bf16),
        ],
        compiler_params=pltpu.CompilerParams(vmem_limit_bytes=40 * 2**20),
        name="k_transform",
    )(x, jnp.asarray(plane_table()), residue)
    w = lax.all_to_all(slots, "ka", 0, 0, tiled=True)
    groups = 3
    out = pl.pallas_call(
        lambda *refs: q_kernel(groups, *refs),
        grid=(5,),
        out_shape=shape((32, 200, MOST), f32),
        in_specs=[
            pl.BlockSpec((32, 100, MOST), lambda i: (0, 0, 0)),
            pl.BlockSpec((512, 256), lambda i: (0, 0)),
            pl.BlockSpec((READERS, MOST), lambda i: (0, 0)),
        ],
        out_specs=pl.BlockSpec((32, 16 * groups, MOST), lambda i: (0, i, 0)),
        scratch_shapes=[pltpu.VMEM((32, 120, MOST), f32)],
        compiler_params=pltpu.CompilerParams(
            dimension_semantics=("arbitrary",), vmem_limit_bytes=40 * 2**20
        ),
        name="q_transform",
    )(w, kron, inverse)
    return out.reshape(32, 100, 2, MOST).transpose(0, 2, 1, 3)


def solution(mesh):
    in_specs = (
        P("pb", "ka", None, None),
        P("ka", None, None),
        P("pb", "ka", None, None),
        P(),
        P(),
        P(),
        P(),
    )
    out_specs = P(None, None, "pb", "ka")
    return jax.shard_map(
        per_device, mesh=mesh, in_specs=in_specs, out_specs=out_specs, check_vma=False
    )
```
